32 devices in a mesh: aux: 16 (over z, y, core), occ: 2 (over x).
Axes of the slice: x: 2, y: 2, z: 4, core: 2. Of those that a mesh axis runs over, the one named last changes fastest.
Arguments:
- factors: bfloat16 [4, 8192, 768], P('occ', 'aux'), may hold values from -0.875 to 0.875
- occ_energy: bfloat16 [4], P('occ'), may hold values from -2 to -0.29882812
- virt_energy: float32 [768], replicated, may hold values from 0.2 to 3
- pairs: int32 [2, 2], P('occ'), may hold values from 0 to 3, as said below
Outputs:
- density: bfloat16 [2, 2, 8192, 768], P('occ', None, 'aux')
The draws below stay inside these ranges and needn't reach their ends.
Inputs may be any that keep to these rules, and one draw needn't show every extreme that they name: Group g's first orbital pairs[g, 0] is one of the 2 orbitals held at index g of occ; the slab distances (pairs[g, 1] // 2 - g) modulo 2 are all different over the groups.
All inputs are finite; a program needn't handle non-finite values.
Results may differ from the reference program's by a relative error of at most 0.0048.
Values may be sent and summed in bfloat16 or wider, within the bound.
A program may use at most 64 MiB of HBM per device.

```python
import jax
import jax.numpy as jnp
from jax import lax

V = 768
OCC_DEV = 2
NAUX = 8192
NOCC = 4
PAIRS = 2


def draw_pairs(key, part):
    subkeys = jax.random.split(jax.random.fold_in(key, 17), 4)
    groups = jnp.arange(PAIRS, dtype=jnp.int32)
    inner_first = jax.random.randint(subkeys[0], (PAIRS,), 0, OCC_DEV, dtype=jnp.int32)
    inner_first = jnp.where(groups == 0, 0, jnp.where(groups == PAIRS - 1, OCC_DEV - 1, inner_first)).astype(jnp.int32)
    inner_second = jax.random.randint(subkeys[1], (PAIRS,), 0, OCC_DEV, dtype=jnp.int32)
    inner_second = jnp.where(groups == PAIRS - 1, OCC_DEV - 1, inner_second).astype(jnp.int32)
    stride = 2 * jax.random.randint(subkeys[2], (), 0, max(PAIRS // 2, 1), dtype=jnp.int32) + 1
    offset = jax.random.randint(subkeys[3], (), 0, PAIRS, dtype=jnp.int32)
    distance = (stride * groups + offset) % PAIRS
    first_orbital = groups * OCC_DEV + inner_first
    second_orbital = (groups + distance) % PAIRS * OCC_DEV + inner_second
    return jnp.stack([first_orbital, second_orbital], axis=1).astype(jnp.int32)


def with_spikes(result, rng, source, target, parts, factor):
    owner, partner = [(jnp.arange(result.shape[position]) // (result.shape[position] // parts)).reshape([-1 if axis == position else 1 for axis in range(result.ndim)]) for position in (source, target)]
    chosen = jax.random.permutation(rng, parts)[partner]
    strong = (owner == chosen) | (owner == (partner + parts // 2) % parts)
    return jnp.where(strong, factor * result, result)


def level_of(rng, dims, pieces, smallest, largest):
    def one(position, blocks):
        heights = jax.random.uniform(jax.random.fold_in(jax.random.fold_in(rng, 6), position), (blocks,), jnp.float32, smallest / len(pieces), largest / len(pieces))
        return jnp.repeat(jnp.exp(heights), dims[position] // blocks).reshape((-1,) + (1,) * (len(dims) - position - 1))

    loudness = one(*pieces[0])
    for cut in pieces[1:]:
        loudness = loudness * one(*cut)
    return loudness


def bell_draw_with(key, extent, scale, reach, shards, heavy, held_as=jnp.bfloat16):
    array = scale * jax.random.normal(key, extent, jnp.float32)
    if shards:
        array = array * level_of(key, extent, shards, -0.22, 0.18)
    return jnp.clip(with_spikes(array, jax.random.fold_in(key, 3), *heavy), -reach, reach).astype(held_as)


def setup_inputs(seed: int = 0) -> dict:
    arg_keys = jax.random.split(jax.random.key(seed), 5)
    factors = bell_draw_with(arg_keys[0], (NOCC, NAUX, V), (NAUX ** -0.25), 0.875, ((0, 2), (1, 16)), (1, 2, 16, 2.0))
    occ_energy = jnp.clip(-2.0 + 1.7011719 * jax.random.uniform(arg_keys[1], (NOCC,), jnp.float32) ** level_of(arg_keys[1], (NOCC,), ((0, 2),), -0.2, 0.2), -2.0, -0.29882812).astype(jnp.bfloat16)
    virt_energy = jnp.clip(jax.random.uniform(arg_keys[2], (V,), jnp.float32, 0.2, 3.0), 0.2, 3.0)
    pairs = draw_pairs(jax.random.fold_in(arg_keys[4], 71), 0)
    return dict(factors=factors, occ_energy=occ_energy, virt_energy=virt_energy, pairs=pairs)


def reference(factors, occ_energy, virt_energy, pairs):
    def pair_density(pair_row):
        first_rows = lax.dynamic_index_in_dim(factors, pair_row[0], 0, keepdims=False)
        second_rows = lax.dynamic_index_in_dim(factors, pair_row[1], 0, keepdims=False)
        first_energy = lax.dynamic_index_in_dim(occ_energy, pair_row[0], 0, keepdims=False).astype(jnp.float32)
        second_energy = lax.dynamic_index_in_dim(occ_energy, pair_row[1], 0, keepdims=False).astype(jnp.float32)
        integrals = lax.dot_general(first_rows, second_rows, (((0,), (0,)), ((), ())), preferred_element_type=jnp.float32)
        denominator = first_energy + second_energy - virt_energy[:, None] - virt_energy[None, :]
        amplitudes = ((2.0 * integrals - integrals.T) / denominator).astype(jnp.bfloat16)
        first_density = lax.dot_general(second_rows, amplitudes, (((1,), (1,)), ((), ())), preferred_element_type=jnp.float32)
        second_density = jnp.dot(first_rows, amplitudes, preferred_element_type=jnp.float32)
        return jnp.stack([first_density, second_density]).astype(jnp.bfloat16)

    return lax.map(pair_density, pairs)
```

```python
import functools

import jax
import jax.numpy as jnp
from jax import lax
from jax.experimental import pallas as pl
from jax.experimental.pallas import tpu as pltpu
from jax.sharding import PartitionSpec as P

LANES = 128
CORES = 2
ROWS_Y = 2
WIDTH = 256
MESH = pl.DeviceIdType.MESH
F32 = jnp.float32
BF16 = jnp.bfloat16


def plan_of(columns, layers):
    strips = columns // WIDTH
    chunks = [[s] for s in range(strips)]
    if any((s + 1) * WIDTH % (ROWS_Y * layers * 16) for s in range(strips)):
        chunks = [list(range(strips))]
    stages = ["X", "C", "Y", "Z", "AZ", "AY", "AC"]
    if len(chunks) == 3:
        order = [(0, "X"), (0, "C"), (0, "Y"), (1, "X"), (0, "Z"), (1, "C"), (0, "AZ")]
        order += [(1, "Y"), (2, "X"), (0, "AY"), (2, "C"), (1, "Z"), (0, "AC"), (2, "Y")]
        order += [(1, "AZ"), (2, "Z"), (1, "AY"), (2, "AZ"), (1, "AC"), (2, "AY"), (2, "AC")]
    else:
        order = [(k, s) for s in stages for k in range(len(chunks))]
    return chunks, order


def layout_of(chunk, layers):
    rows = sum((s + 1) * WIDTH for s in chunk)
    return rows, rows // (ROWS_Y * layers)


def body(groups, layers, pairs_ref, msg_ref, virt_ref, f_hbm, out_ref, *scratch):
    scratch = list(scratch)
    take = lambda: scratch.pop(0)
    slab, depth, columns = f_hbm.shape
    chunks, order = plan_of(columns, layers)
    f_ref, msgs, stage, bi, bj, acc = [take() for _ in range(6)]
    slots = [take() for _ in range(columns // WIDTH)]
    per_chunk = [[take() for _ in range(9)] for _ in chunks]
    (f_sem, m_send, m_recv, x_send, x_recv, c_sem, y_sem, z_send, z_recv, az_send, az_recv, ay_sem, ac_sem) = [
        take() for _ in range(13)
    ]

    aux = lax.axis_index("aux")
    occ = lax.axis_index("occ")
    core = lax.rem(aux, CORES)
    row = lax.rem(aux // CORES, ROWS_Y)
    layer = aux // (CORES * ROWS_Y)

    def device(z, y, c, g):
        return {"aux": (z * ROWS_Y + y) * CORES + c, "occ": g}

    core_peer = device(layer, row, 1 - core, occ)
    row_peer = device(layer, 1 - row, core, occ)
    layer_peer = lambda j: device(lax.rem(layer + j, layers), row, core, occ)
    occ_peer = lambda d: {"aux": aux, "occ": lax.rem(occ + groups - d, groups)}

    load = pltpu.make_async_copy(f_hbm, f_ref, f_sem)
    load.start()
    barrier = pltpu.get_barrier_semaphore()
    peers = [core_peer, row_peer]
    peers += [layer_peer(j) for j in range(1, layers)]
    peers += [occ_peer(d) for d in range(1, groups)]
    for peer in peers:
        pl.semaphore_signal(barrier, inc=1, device_id=peer, device_id_type=MESH)
    pl.semaphore_wait(barrier, len(peers))

    started = []

    def send(src, dst, send_sem, recv_sem, peer):
        copy = pltpu.make_async_remote_copy(
            src_ref=src, dst_ref=dst, send_sem=send_sem, recv_sem=recv_sem, device_id=peer, device_id_type=MESH
        )
        copy.start()
        started.append(copy)
        return copy

    def landed(ref, send_sem, recv_sem, peer):
        pltpu.make_async_remote_copy(
            src_ref=ref, dst_ref=ref, send_sem=send_sem, recv_sem=recv_sem, device_id=peer, device_id_type=MESH
        ).wait_recv()

    sent = [send(msg_ref, msgs.at[d], m_send.at[d], m_recv.at[d], occ_peer(d)) for d in range(1, groups)]
    msgs[0] = msg_ref[...]
    load.wait()
    i_local = lax.rem(pairs_ref[0, 0], slab)
    j_slab = pairs_ref[0, 1] // slab
    j_local = pairs_ref[0, 1] - j_slab * slab
    distance = lax.rem(j_slab - occ + groups, groups)
    for d in range(1, groups):
        sent[d - 1].wait_recv()
    strips = columns // WIDTH
    for s in range(strips):
        cols = slice(s * WIDTH, (s + 1) * WIDTH)
        for d in range(1, groups):
            asked = msgs[groups - d]
            rows = jnp.zeros((depth, WIDTH), BF16)
            for o in range(slab):
                mask = jnp.concatenate([asked[o : o + 1]] * (WIDTH // LANES), axis=1).astype(BF16)
                rows = rows + f_ref[o, :, cols] * mask
            stage[d - 1, s] = rows
            send(stage.at[d - 1, s], slots[s].at[d], x_send.at[d, s], x_recv.at[d, s], occ_peer(d))
    for s in range(strips):
        cols = slice(s * WIDTH, (s + 1) * WIDTH)
        slots[s][0] = f_ref[j_local, :, cols]
    bi[...] = f_ref[i_local]
    energy = msgs[0, pl.ds(slab + i_local, 1), :] + msgs[distance, pl.ds(slab + j_local, 1), :]

    down = []
    for t in range(columns // LANES):
        down.append(jnp.broadcast_to(virt_ref[t : t + 1, :], (LANES, LANES)).T)
    for k, chunk in enumerate(chunks):
        v_rows, v_lanes = per_chunk[k][7:9]
        base = 0
        for s in chunk:
            size = (s + 1) * WIDTH
            for t in range(size // LANES):
                v_rows[base + t * LANES : base + (t + 1) * LANES, :] = down[t]
            for c in range(CORES):
                index = s * (WIDTH // LANES) + c
                v_lanes[c, base : base + size, :] = jnp.broadcast_to(virt_ref[index : index + 1, :], (size, LANES))
            base += size

    def over_q(left, right):
        return lax.dot_general(left, right, (((0,), (0,)), ((), ())), preferred_element_type=F32)

    pending = {}

    def run_stage(k, name):
        chunk = chunks[k]
        part, give, got_c, give_y, got_y, give_z, amp, v_rows, v_lanes = per_chunk[k]
        rows, block = layout_of(chunk, layers)
        if name == "X":
            base = 0
            for s in chunk:
                end = (s + 1) * WIDTH
                cols = slice(s * WIDTH, end)
                for d in range(1, groups):
                    landed(slots[s].at[d], x_send.at[d, s], x_recv.at[d, s], occ_peer(d))
                bj[:, cols] = slots[s][distance]
                for w in range(2):
                    left, right = (bi, bj) if w == 0 else (bj, bi)
                    value = over_q(left[:, :end], right[:, cols])
                    for c in range(CORES):
                        part[c, w, base : base + end, :] = value[:, c * LANES : (c + 1) * LANES]
                base += end
            give[...] = part[1 - core].astype(BF16)
            pending[k, "C"] = send(give, got_c, c_sem.at[0, k], c_sem.at[1, k], core_peer)
        elif name == "C":
            pending[k, "C"].wait_recv()
            half = rows // ROWS_Y
            there = pl.ds(pl.multiple_of((1 - row) * half, half), half)
            here = pl.ds(pl.multiple_of(row * half, half), half)
            give_y[...] = (part[core, :, there, :] + got_c[:, there, :].astype(F32)).astype(BF16)
            pending[k, "Y"] = send(give_y, got_y, y_sem.at[0, k], y_sem.at[1, k], row_peer)
            part[0, :, 0:half, :] = part[core, :, here, :] + got_c[:, here, :].astype(F32)
        elif name == "Y":
            pending[k, "Y"].wait_recv()
            for j in range(1, layers):
                z = lax.rem(layer + j, layers)
                there = pl.ds(pl.multiple_of(z * block, block), block)
                give_z[0, j] = (part[0, :, there, :] + got_y[:, there, :].astype(F32)).astype(BF16)
                send(give_z.at[0, j], give_z.at[1, j], z_send.at[k, j], z_recv.at[k, j], layer_peer(j))
        elif name == "Z":
            here = pl.ds(pl.multiple_of(layer * block, block), block)
            total = part[0, :, here, :] + got_y[:, here, :].astype(F32)
            for j in range(1, layers):
                landed(give_z.at[1, j], z_send.at[k, j], z_recv.at[k, j], layer_peer(j))
                total = total + give_z[1, j].astype(F32)
            mine = pl.ds(pl.multiple_of((row * layers + layer) * block, block), block)
            down_rows = v_rows[mine, :]
            along = v_lanes[core, mine, :]
            first = (2.0 * total[0] - total[1]) / (energy - down_rows - along)
            second = (2.0 * total[1] - total[0]) / (energy - along - down_rows)
            amp[core, row, layer, 0] = first.astype(BF16)
            amp[core, row, layer, 1] = second.astype(BF16)
            home = amp.at[core, row, layer]
            for j in range(1, layers):
                send(home, home, az_send.at[k, j], az_recv.at[k, j], layer_peer(j))
        elif name == "AZ":
            for j in range(1, layers):
                z = lax.rem(layer + layers - j, layers)
                landed(amp.at[core, row, z], az_send.at[k, j], az_recv.at[k, j], layer_peer(j))
            home = amp.at[core, row]
            send(home, home, ay_sem.at[0, k], ay_sem.at[1, k], row_peer)
        elif name == "AY":
            landed(amp.at[core, 1 - row], ay_sem.at[0, k], ay_sem.at[1, k], row_peer)
            home = amp.at[core]
            send(home, home, ac_sem.at[0, k], ac_sem.at[1, k], core_peer)
        else:
            landed(amp.at[1 - core], ac_sem.at[0, k], ac_sem.at[1, k], core_peer)
            base = 0
            whole = []
            for w in range(2):
                halves = [amp[c, :, :, w].reshape(rows, LANES) for c in range(CORES)]
                whole.append(jnp.concatenate(halves, axis=1))
            for s in chunk:
                start, end = s * WIDTH, (s + 1) * WIDTH
                cols = slice(start, end)
                for w in range(2):
                    b = bj if w == 0 else bi
                    plain = whole[1 - w][base : base + end]
                    acc[w, :, cols] = jnp.dot(b[:, :end], plain, preferred_element_type=F32)
                    if start:
                        turned = whole[w][base : base + start]
                        acc[w, :, :start] += lax.dot_general(
                            b[:, cols], turned, (((1,), (1,)), ((), ())), preferred_element_type=F32
                        )
                base += end

    for k, name in order:
        run_stage(k, name)
    out_ref[...] = acc[...].astype(BF16)
    for copy in started:
        copy.wait_send()


def on_device(mesh_shape, factors, occ_energy, virt_energy, pairs):
    groups = mesh_shape["occ"]
    layers = mesh_shape["aux"] // (CORES * ROWS_Y)
    slab, depth, columns = factors.shape
    chunks, _ = plan_of(columns, layers)
    strips = columns // WIDTH
    asked = (jnp.arange(slab) == pairs[0, 1] % slab).astype(F32)
    msg = jnp.concatenate([asked, occ_energy.astype(F32)])
    msg = jnp.broadcast_to(msg[:, None], (2 * slab, LANES))
    scratch = [
        pltpu.VMEM((slab, depth, columns), BF16),
        pltpu.VMEM((groups, 2 * slab, LANES), F32),
        pltpu.VMEM((groups - 1, strips, depth, WIDTH), BF16),
        pltpu.VMEM((depth, columns), BF16),
        pltpu.VMEM((depth, columns), BF16),
        pltpu.VMEM((2, depth, columns), F32),
    ]
    scratch += [pltpu.VMEM((groups, depth, WIDTH), BF16)] * strips
    for chunk in chunks:
        rows, block = layout_of(chunk, layers)
        scratch += [
            pltpu.VMEM((CORES, 2, rows, LANES), F32),
            pltpu.VMEM((2, rows, LANES), BF16),
            pltpu.VMEM((2, rows, LANES), BF16),
            pltpu.VMEM((2, rows // ROWS_Y, LANES), BF16),
            pltpu.VMEM((2, rows // ROWS_Y, LANES), BF16),
            pltpu.VMEM((2, layers, 2, block, LANES), BF16),
            pltpu.VMEM((CORES, ROWS_Y, layers, 2, block, LANES), BF16),
            pltpu.VMEM((rows, LANES), F32),
            pltpu.VMEM((CORES, rows, LANES), F32),
        ]
    n = len(chunks)
    dma = pltpu.SemaphoreType.DMA
    scratch += [dma(())]
    scratch += [dma((groups,))] * 2
    scratch += [dma((groups, strips))] * 2
    scratch += [dma((2, n))] * 2
    scratch += [dma((n, layers))] * 4
    scratch += [dma((2, n))] * 2
    vmem = pl.BlockSpec(memory_space=pltpu.VMEM)
    out = pl.pallas_call(
        functools.partial(body, groups, layers),
        out_shape=jax.ShapeDtypeStruct((2, depth, columns), BF16),
        in_specs=[pl.BlockSpec(memory_space=pltpu.SMEM), vmem, vmem, pl.BlockSpec(memory_space=pl.ANY)],
        out_specs=vmem,
        scratch_shapes=scratch,
        compiler_params=pltpu.CompilerParams(
            collective_id=0, has_side_effects=True, vmem_limit_bytes=60 * 1024 * 1024
        ),
    )(pairs, msg, virt_energy.reshape(columns // LANES, LANES), factors)
    return out[None]


def solution(mesh):
    in_specs = (P("occ", "aux", None), P("occ"), P(), P("occ", None))
    out_specs = P("occ", None, "aux", None)
    return jax.shard_map(
        functools.partial(on_device, dict(mesh.shape)),
        mesh=mesh,
        in_specs=in_specs,
        out_specs=out_specs,
        check_vma=False,
    )
```

```python
import functools

import jax
import jax.numpy as jnp
from jax import lax
from jax.experimental import pallas as pl
from jax.experimental.pallas import tpu as pltpu
from jax.sharding import PartitionSpec as P

LANES = 128
GRANT = 40 * 1024 * 1024
CORES = 2
ROWS_Y = 2
MESH = pl.DeviceIdType.MESH
F32 = jnp.float32
BF16 = jnp.bfloat16


def plan_of(columns, layers):
    strips = columns // LANES
    unit = CORES * ROWS_Y * layers * 16

    def fit(members):
        sizes = [(s + 1) * LANES for s in members]
        for at in reversed(range(len(members))):
            while sum(sizes) % unit and sizes[at] < columns:
                sizes[at] += LANES
        return [(s, (s + 1) * LANES, size) for s, size in zip(members, sizes)]

    split = [list(range(strips // 2))] + [[s] for s in range(strips // 2, strips)]
    chunks = [fit(members) for members in split]
    if any(sum(size for _, _, size in chunk) % unit for chunk in chunks):
        chunks = [fit(list(range(strips)))]
    stages = ["X", "C", "Y", "Z", "AZ", "AY", "AC"]
    when = {"X": 9, "C": 11, "Y": 15, "Z": 19, "AZ": 23, "AY": 27, "AC": 28}
    order = sorted((when[s] + 3 * k, k, stages.index(s), s) for s in stages for k in range(len(chunks)))
    return chunks, [(k, s) for _, k, _, s in order]


def layout_of(chunk, layers):
    rows = sum(size for _, _, size in chunk)
    return rows, rows // (CORES * ROWS_Y * layers)


def body(groups, layers, pairs_ref, energy_ref, virt_ref, f_hbm, out_ref, *scratch):
    scratch = list(scratch)
    take = lambda: scratch.pop(0)
    slab, depth, columns = f_hbm.shape
    chunks, order = plan_of(columns, layers)
    f_ref, msgs, bi, bj, bi_t, bj_t, acc = [take() for _ in range(7)]
    per_chunk = [[take() for _ in range(11)] for _ in chunks]
    (f_sem, m_send, m_recv, x_send, x_recv, c_sem, y_sem, z_send, z_recv, az_send, az_recv, ay_sem, ac_sem) = [
        take() for _ in range(13)
    ]

    aux = lax.axis_index("aux")
    occ = lax.axis_index("occ")
    core = lax.rem(aux, CORES)
    row = lax.rem(aux // CORES, ROWS_Y)
    layer = aux // (CORES * ROWS_Y)

    def device(z, y, c, g):
        return {"aux": (z * ROWS_Y + y) * CORES + c, "occ": g}

    core_peer = device(layer, row, 1 - core, occ)
    row_peer = device(layer, 1 - row, core, occ)
    layer_peer = lambda j: device(lax.rem(layer + j, layers), row, core, occ)
    occ_peer = lambda d: {"aux": aux, "occ": lax.rem(occ + groups - d, groups)}

    load = pltpu.make_async_copy(f_hbm, f_ref, f_sem)
    load.start()
    barrier = pltpu.get_barrier_semaphore()
    peers = [core_peer, row_peer]
    peers += [layer_peer(j) for j in range(1, layers)]
    peers += [occ_peer(d) for d in range(1, groups)]
    for peer in peers:
        pl.semaphore_signal(barrier, inc=1, device_id=peer, device_id_type=MESH)
    pl.semaphore_wait(barrier, len(peers))

    started = []

    def send(src, dst, send_sem, recv_sem, peer):
        copy = pltpu.make_async_remote_copy(
            src_ref=src, dst_ref=dst, send_sem=send_sem, recv_sem=recv_sem, device_id=peer, device_id_type=MESH
        )
        copy.start()
        started.append(copy)
        return copy

    def landed(ref, send_sem, recv_sem, peer):
        pltpu.make_async_remote_copy(
            src_ref=ref, dst_ref=ref, send_sem=send_sem, recv_sem=recv_sem, device_id=peer, device_id_type=MESH
        ).wait_recv()

    i_local = lax.rem(pairs_ref[0, 0], slab)
    j_slab = pairs_ref[0, 1] // slab
    j_local = pairs_ref[0, 1] - j_slab * slab
    distance = lax.rem(j_slab - occ + groups, groups)
    slab_energy = energy_ref[...].astype(F32)
    for o in range(slab):
        wants = jnp.where(j_local == o, 1.0, 0.0).astype(F32)
        msgs[0, o : o + 1, :] = jnp.full((1, LANES), wants, F32)
        msgs[0, slab + o : slab + o + 1, :] = jnp.broadcast_to(slab_energy[:, o : o + 1], (1, LANES))
    sent = [send(msgs.at[0], msgs.at[d], m_send.at[d], m_recv.at[d], occ_peer(d)) for d in range(1, groups)]
    load.wait()
    for d in range(1, groups):
        sent[d - 1].wait_recv()

    def columns_of(chunk):
        return slice(chunk[0][0] * LANES, chunk[-1][1])

    for k, chunk in enumerate(chunks):
        cols = columns_of(chunk)
        stage, slots = per_chunk[k][9:11]
        for d in range(1, groups):
            asked = msgs[groups - d]
            rows = jnp.zeros((depth, cols.stop - cols.start), BF16)
            for o in range(slab):
                mask = jnp.concatenate([asked[o : o + 1]] * len(chunk), axis=1).astype(BF16)
                rows = rows + f_ref[o, :, cols] * mask
            stage[d - 1] = rows
            send(stage.at[d - 1], slots.at[d], x_send.at[d, k], x_recv.at[d, k], occ_peer(d))
    for k, chunk in enumerate(chunks):
        per_chunk[k][10][0] = f_ref[j_local, :, columns_of(chunk)]
    bi[...] = f_ref[i_local]
    bi_t[...] = bi[...].T
    energy = msgs[0, pl.ds(slab + i_local, 1), :] + msgs[distance, pl.ds(slab + j_local, 1), :]

    down = []
    for t in range(columns // LANES):
        down.append(jnp.broadcast_to(virt_ref[t : t + 1, :], (LANES, LANES)).T)
    for k, chunk in enumerate(chunks):
        part, v_rows, v_lanes = per_chunk[k][0], *per_chunk[k][7:9]
        base = 0
        for s, end, size in chunk:
            for t in range(size // LANES):
                v_rows[base + t * LANES : base + (t + 1) * LANES, :] = down[t]
            v_lanes[base : base + size, :] = jnp.broadcast_to(virt_ref[s : s + 1, :], (size, LANES))
            if size > end:
                part[:, base + end : base + size, :] = jnp.zeros((2, size - end, LANES), F32)
            base += size

    pending = {}

    def run_stage(k, name):
        chunk = chunks[k]
        part, give, got_c, give_y, got_y, give_z, amp, v_rows, v_lanes, stage, slots = per_chunk[k]
        rows, block = layout_of(chunk, layers)
        half, quarter = rows // CORES, rows // (CORES * ROWS_Y)

        def span(index, size):
            return pl.ds(pl.multiple_of(index * size, size), size)

        if name == "X":
            for d in range(1, groups):
                landed(slots.at[d], x_send.at[d, k], x_recv.at[d, k], occ_peer(d))
            cols = columns_of(chunk)
            arrived = slots[distance]
            bj[:, cols] = arrived
            bj_t[cols, :] = arrived.T
            base = 0
            for s, end, size in chunk:
                cols = slice(s * LANES, end)
                part[0, base : base + end, :] = jnp.dot(bi_t[:end, :], bj[:, cols], preferred_element_type=F32)
                part[1, base : base + end, :] = jnp.dot(bj_t[:end, :], bi[:, cols], preferred_element_type=F32)
                base += size
            give[...] = part[:, span(1 - core, half), :].astype(BF16)
            pending[k, "C"] = send(give, got_c, c_sem.at[0, k], c_sem.at[1, k], core_peer)
        elif name == "C":
            pending[k, "C"].wait_recv()
            there = span(core * ROWS_Y + 1 - row, quarter)
            here = span(core * ROWS_Y + row, quarter)
            give_y[...] = (part[:, there, :] + got_c[:, span(1 - row, quarter), :].astype(F32)).astype(BF16)
            pending[k, "Y"] = send(give_y, got_y, y_sem.at[0, k], y_sem.at[1, k], row_peer)
            part[:, here, :] = part[:, here, :] + got_c[:, span(row, quarter), :].astype(F32)
        elif name == "Y":
            pending[k, "Y"].wait_recv()
            base = (core * ROWS_Y + row) * layers
            for j in range(1, layers):
                z = lax.rem(layer + j, layers)
                give_z[0, j] = (part[:, span(base + z, block), :] + got_y[:, span(z, block), :].astype(F32)).astype(BF16)
                send(give_z.at[0, j], give_z.at[1, j], z_send.at[k, j], z_recv.at[k, j], layer_peer(j))
        elif name == "Z":
            mine = span((core * ROWS_Y + row) * layers + layer, block)
            total = part[:, mine, :] + got_y[:, span(layer, block), :].astype(F32)
            down_rows = v_rows[mine, :]
            along = v_lanes[mine, :]
            for j in range(1, layers):
                landed(give_z.at[1, j], z_send.at[k, j], z_recv.at[k, j], layer_peer(j))
                total = total + give_z[1, j].astype(F32)
            first = (2.0 * total[0] - total[1]) / (energy - down_rows - along)
            second = (2.0 * total[1] - total[0]) / (energy - along - down_rows)
            amp[core, row, layer, 0] = first.astype(BF16)
            amp[core, row, layer, 1] = second.astype(BF16)
            home = amp.at[core, row, layer]
            for j in range(1, layers):
                send(home, home, az_send.at[k, j], az_recv.at[k, j], layer_peer(j))
        elif name == "AZ":
            for j in range(1, layers):
                z = lax.rem(layer + layers - j, layers)
                landed(amp.at[core, row, z], az_send.at[k, j], az_recv.at[k, j], layer_peer(j))
            home = amp.at[core, row]
            send(home, home, ay_sem.at[0, k], ay_sem.at[1, k], row_peer)
        elif name == "AY":
            landed(amp.at[core, 1 - row], ay_sem.at[0, k], ay_sem.at[1, k], row_peer)
            home = amp.at[core]
            send(home, home, ac_sem.at[0, k], ac_sem.at[1, k], core_peer)
        else:
            landed(amp.at[1 - core], ac_sem.at[0, k], ac_sem.at[1, k], core_peer)
            whole = [amp[:, :, :, w].reshape(rows, LANES) for w in range(2)]
            base = 0
            for s, end, size in chunk:
                start = s * LANES
                cols = slice(start, end)
                last = end == columns
                for w in range(2):
                    b = bj if w == 0 else bi
                    plain = jnp.dot(b[:, :end], whole[1 - w][base : base + end], preferred_element_type=F32)
                    if last:
                        out_ref[w, :, cols] = plain.astype(BF16)
                    else:
                        acc[w, :, cols] = plain
                    if start:
                        turned = lax.dot_general(
                            b[:, cols],
                            whole[w][base : base + start],
                            (((1,), (1,)), ((), ())),
                            preferred_element_type=F32,
                        )
                        if last:
                            out_ref[w, :, :start] = (acc[w, :, :start] + turned).astype(BF16)
                        else:
                            acc[w, :, :start] += turned
                base += size

    for k, name in order:
        run_stage(k, name)
    for copy in started:
        copy.wait_send()


def on_device(mesh_shape, factors, occ_energy, virt_energy, pairs):
    groups = mesh_shape["occ"]
    layers = mesh_shape["aux"] // (CORES * ROWS_Y)
    slab, depth, columns = factors.shape
    chunks, _ = plan_of(columns, layers)
    scratch = [
        pltpu.VMEM((slab, depth, columns), BF16),
        pltpu.VMEM((groups, 2 * slab, LANES), F32),
        pltpu.VMEM((depth, columns), BF16),
        pltpu.VMEM((depth, columns), BF16),
        pltpu.VMEM((columns, depth), BF16),
        pltpu.VMEM((columns, depth), BF16),
        pltpu.VMEM((2, depth, columns), F32),
    ]
    for chunk in chunks:
        rows, block = layout_of(chunk, layers)
        width = len(chunk) * LANES
        scratch += [
            pltpu.VMEM((2, rows, LANES), F32),
            pltpu.VMEM((2, rows // CORES, LANES), BF16),
            pltpu.VMEM((2, rows // CORES, LANES), BF16),
            pltpu.VMEM((2, rows // (CORES * ROWS_Y), LANES), BF16),
            pltpu.VMEM((2, rows // (CORES * ROWS_Y), LANES), BF16),
            pltpu.VMEM((2, layers, 2, block, LANES), BF16),
            pltpu.VMEM((CORES, ROWS_Y, layers, 2, block, LANES), BF16),
            pltpu.VMEM((rows, LANES), F32),
            pltpu.VMEM((rows, LANES), F32),
            pltpu.VMEM((groups - 1, depth, width), BF16),
            pltpu.VMEM((groups, depth, width), BF16),
        ]
    n = len(chunks)
    dma = pltpu.SemaphoreType.DMA
    scratch += [dma(())]
    scratch += [dma((groups,))] * 2
    scratch += [dma((groups, n))] * 2
    scratch += [dma((2, n))] * 2
    scratch += [dma((n, layers))] * 4
    scratch += [dma((2, n))] * 2
    vmem = pl.BlockSpec(memory_space=pltpu.VMEM)
    out = pl.pallas_call(
        functools.partial(body, groups, layers),
        out_shape=jax.ShapeDtypeStruct((2, depth, columns), BF16),
        in_specs=[pl.BlockSpec(memory_space=pltpu.SMEM), vmem, vmem, pl.BlockSpec(memory_space=pl.ANY)],
        out_specs=vmem,
        scratch_shapes=scratch,
        compiler_params=pltpu.CompilerParams(
            collective_id=0, has_side_effects=True, vmem_limit_bytes=GRANT
        ),
    )(pairs, occ_energy[None], virt_energy.reshape(columns // LANES, LANES), factors)
    return out[None]


def solution(mesh):
    in_specs = (P("occ", "aux", None), P("occ"), P(), P("occ", None))
    out_specs = P("occ", None, "aux", None)
    return jax.shard_map(
        functools.partial(on_device, dict(mesh.shape)),
        mesh=mesh,
        in_specs=in_specs,
        out_specs=out_specs,
        check_vma=False,
    )
```

```python
import functools

import jax
import jax.numpy as jnp
from jax import lax
from jax.experimental import pallas as pl
from jax.experimental.pallas import tpu as pltpu
from jax.sharding import PartitionSpec as P

LANES = 128
GRANT = 40 * 1024 * 1024
CORES = 2
ROWS_Y = 2
MESH = pl.DeviceIdType.MESH
F32 = jnp.float32
BF16 = jnp.bfloat16


def plan_of(columns, layers):
    strips = columns // LANES
    unit = CORES * ROWS_Y * layers * 16

    def fit(members):
        sizes = [(s + 1) * LANES for s in members]
        for at in reversed(range(len(members))):
            while sum(sizes) % unit and sizes[at] < columns:
                sizes[at] += LANES
        return [(s, (s + 1) * LANES, size) for s, size in zip(members, sizes)]

    split = [list(range(strips // 2))] + [[s] for s in range(strips // 2, strips)]
    chunks = [fit(members) for members in split]
    if any(sum(size for _, _, size in chunk) % unit for chunk in chunks):
        chunks = [fit(list(range(strips)))]
    stages = ["X", "C", "Y", "Z", "AZ", "AY", "AC"]
    when = {"X": 9, "C": 11, "Y": 15, "Z": 19, "AZ": 23, "AY": 27, "AC": 28}
    order = sorted((when[s] + 3 * k, k, stages.index(s), s) for s in stages for k in range(len(chunks)))
    return chunks, [(k, s) for _, k, _, s in order]


def layout_of(chunk, layers):
    rows = sum(size for _, _, size in chunk)
    return rows, rows // (CORES * ROWS_Y * layers)


def body(groups, layers, pairs_hbm, energy_hbm, virt_hbm, f_hbm, out_ref, *scratch):
    scratch = list(scratch)
    take = lambda: scratch.pop(0)
    slab, depth, columns = f_hbm.shape
    chunks, order = plan_of(columns, layers)
    pairs_ref, energy_ref, virt_ref, small_sem = [take() for _ in range(4)]
    f_ref, msgs, bi, bj, bi_t, bj_t, acc = [take() for _ in range(7)]
    per_chunk = [[take() for _ in range(11)] for _ in chunks]
    (f_sem, m_send, m_recv, x_send, x_recv, c_sem, y_sem, z_send, z_recv, az_send, az_recv, ay_sem, ac_sem) = [
        take() for _ in range(13)
    ]

    aux = lax.axis_index("aux")
    occ = lax.axis_index("occ")
    core = lax.rem(aux, CORES)
    row = lax.rem(aux // CORES, ROWS_Y)
    layer = aux // (CORES * ROWS_Y)

    def device(z, y, c, g):
        return {"aux": (z * ROWS_Y + y) * CORES + c, "occ": g}

    core_peer = device(layer, row, 1 - core, occ)
    row_peer = device(layer, 1 - row, core, occ)
    layer_peer = lambda j: device(lax.rem(layer + j, layers), row, core, occ)
    occ_peer = lambda d: {"aux": aux, "occ": lax.rem(occ + groups - d, groups)}

    def columns_of(chunk):
        return slice(chunk[0][0] * LANES, chunk[-1][1])

    small = []
    for at, (src, dst) in enumerate([(pairs_hbm, pairs_ref), (energy_hbm, energy_ref), (virt_hbm, virt_ref)]):
        small.append(pltpu.make_async_copy(src, dst, small_sem.at[at]))
        small[at].start()
    loads = []
    for k, chunk in enumerate(chunks):
        cols = columns_of(chunk)
        loads.append(pltpu.make_async_copy(f_hbm.at[:, :, cols], f_ref.at[:, :, cols], f_sem.at[k]))
        loads[k].start()
    barrier = pltpu.get_barrier_semaphore()
    peers = [core_peer, row_peer]
    peers += [layer_peer(j) for j in range(1, layers)]
    peers += [occ_peer(d) for d in range(1, groups)]
    for peer in peers:
        pl.semaphore_signal(barrier, inc=1, device_id=peer, device_id_type=MESH)
    pl.semaphore_wait(barrier, len(peers))

    started = []

    def send(src, dst, send_sem, recv_sem, peer):
        copy = pltpu.make_async_remote_copy(
            src_ref=src, dst_ref=dst, send_sem=send_sem, recv_sem=recv_sem, device_id=peer, device_id_type=MESH
        )
        copy.start()
        started.append(copy)
        return copy

    def landed(ref, send_sem, recv_sem, peer):
        pltpu.make_async_remote_copy(
            src_ref=ref, dst_ref=ref, send_sem=send_sem, recv_sem=recv_sem, device_id=peer, device_id_type=MESH
        ).wait_recv()

    for copy in small:
        copy.wait()
    i_local = lax.rem(pairs_ref[0, 0], slab)
    j_slab = pairs_ref[0, 1] // slab
    j_local = pairs_ref[0, 1] - j_slab * slab
    distance = lax.rem(j_slab - occ + groups, groups)
    slab_energy = energy_ref[...].astype(F32)
    for o in range(slab):
        wants = jnp.where(j_local == o, 1.0, 0.0).astype(F32)
        msgs[0, o : o + 1, :] = jnp.full((1, LANES), wants, F32)
        msgs[0, slab + o : slab + o + 1, :] = jnp.broadcast_to(slab_energy[:, o : o + 1], (1, LANES))
    sent = [send(msgs.at[0], msgs.at[d], m_send.at[d], m_recv.at[d], occ_peer(d)) for d in range(1, groups)]
    for d in range(1, groups):
        sent[d - 1].wait_recv()

    for k, chunk in enumerate(chunks):
        loads[k].wait()
        cols = columns_of(chunk)
        stage, slots = per_chunk[k][9:11]
        for d in range(1, groups):
            asked = msgs[groups - d]
            rows = jnp.zeros((depth, cols.stop - cols.start), BF16)
            for o in range(slab):
                mask = jnp.concatenate([asked[o : o + 1]] * len(chunk), axis=1).astype(BF16)
                rows = rows + f_ref[o, :, cols] * mask
            stage[d - 1] = rows
            send(stage.at[d - 1], slots.at[d], x_send.at[d, k], x_recv.at[d, k], occ_peer(d))
    for k, chunk in enumerate(chunks):
        per_chunk[k][10][0] = f_ref[j_local, :, columns_of(chunk)]
    bi[...] = f_ref[i_local]
    bi_t[...] = bi[...].T
    energy = msgs[0, pl.ds(slab + i_local, 1), :] + msgs[distance, pl.ds(slab + j_local, 1), :]

    down = []
    for t in range(columns // LANES):
        down.append(jnp.broadcast_to(virt_ref[t : t + 1, :], (LANES, LANES)).T)
    for k, chunk in enumerate(chunks):
        part, v_rows, v_lanes = per_chunk[k][0], *per_chunk[k][7:9]
        base = 0
        for s, end, size in chunk:
            for t in range(size // LANES):
                v_rows[base + t * LANES : base + (t + 1) * LANES, :] = down[t]
            v_lanes[base : base + size, :] = jnp.broadcast_to(virt_ref[s : s + 1, :], (size, LANES))
            if size > end:
                part[:, base + end : base + size, :] = jnp.zeros((2, size - end, LANES), F32)
            base += size

    pending = {}

    def run_stage(k, name):
        chunk = chunks[k]
        part, give, got_c, give_y, got_y, give_z, amp, v_rows, v_lanes, stage, slots = per_chunk[k]
        rows, block = layout_of(chunk, layers)
        half, quarter = rows // CORES, rows // (CORES * ROWS_Y)

        def span(index, size):
            return pl.ds(pl.multiple_of(index * size, size), size)

        if name == "X":
            for d in range(1, groups):
                landed(slots.at[d], x_send.at[d, k], x_recv.at[d, k], occ_peer(d))
            cols = columns_of(chunk)
            arrived = slots[distance]
            bj[:, cols] = arrived
            bj_t[cols, :] = arrived.T
            base = 0
            for s, end, size in chunk:
                cols = slice(s * LANES, end)
                part[0, base : base + end, :] = jnp.dot(bi_t[:end, :], bj[:, cols], preferred_element_type=F32)
                part[1, base : base + end, :] = jnp.dot(bj_t[:end, :], bi[:, cols], preferred_element_type=F32)
                base += size
            give[...] = part[:, span(1 - core, half), :].astype(BF16)
            pending[k, "C"] = send(give, got_c, c_sem.at[0, k], c_sem.at[1, k], core_peer)
        elif name == "C":
            pending[k, "C"].wait_recv()
            there = span(core * ROWS_Y + 1 - row, quarter)
            here = span(core * ROWS_Y + row, quarter)
            give_y[...] = (part[:, there, :] + got_c[:, span(1 - row, quarter), :].astype(F32)).astype(BF16)
            pending[k, "Y"] = send(give_y, got_y, y_sem.at[0, k], y_sem.at[1, k], row_peer)
            part[:, here, :] = part[:, here, :] + got_c[:, span(row, quarter), :].astype(F32)
        elif name == "Y":
            pending[k, "Y"].wait_recv()
            base = (core * ROWS_Y + row) * layers
            for j in range(1, layers):
                z = lax.rem(layer + j, layers)
                give_z[0, j] = (part[:, span(base + z, block), :] + got_y[:, span(z, block), :].astype(F32)).astype(BF16)
                send(give_z.at[0, j], give_z.at[1, j], z_send.at[k, j], z_recv.at[k, j], layer_peer(j))
        elif name == "Z":
            mine = span((core * ROWS_Y + row) * layers + layer, block)
            total = part[:, mine, :] + got_y[:, span(layer, block), :].astype(F32)
            down_rows = v_rows[mine, :]
            along = v_lanes[mine, :]
            for j in range(1, layers):
                landed(give_z.at[1, j], z_send.at[k, j], z_recv.at[k, j], layer_peer(j))
                total = total + give_z[1, j].astype(F32)
            first = (2.0 * total[0] - total[1]) / (energy - down_rows - along)
            second = (2.0 * total[1] - total[0]) / (energy - along - down_rows)
            amp[core, row, layer, 0] = first.astype(BF16)
            amp[core, row, layer, 1] = second.astype(BF16)
            home = amp.at[core, row, layer]
            for j in range(1, layers):
                send(home, home, az_send.at[k, j], az_recv.at[k, j], layer_peer(j))
        elif name == "AZ":
            for j in range(1, layers):
                z = lax.rem(layer + layers - j, layers)
                landed(amp.at[core, row, z], az_send.at[k, j], az_recv.at[k, j], layer_peer(j))
            home = amp.at[core, row]
            send(home, home, ay_sem.at[0, k], ay_sem.at[1, k], row_peer)
        elif name == "AY":
            landed(amp.at[core, 1 - row], ay_sem.at[0, k], ay_sem.at[1, k], row_peer)
            home = amp.at[core]
            send(home, home, ac_sem.at[0, k], ac_sem.at[1, k], core_peer)
        else:
            landed(amp.at[1 - core], ac_sem.at[0, k], ac_sem.at[1, k], core_peer)
            whole = [amp[:, :, :, w].reshape(rows, LANES) for w in range(2)]
            base = 0
            for s, end, size in chunk:
                start = s * LANES
                cols = slice(start, end)
                last = end == columns
                for w in range(2):
                    b = bj if w == 0 else bi
                    plain = jnp.dot(b[:, :end], whole[1 - w][base : base + end], preferred_element_type=F32)
                    if last:
                        out_ref[w, :, cols] = plain.astype(BF16)
                    else:
                        acc[w, :, cols] = plain
                    if start:
                        turned = lax.dot_general(
                            b[:, cols],
                            whole[w][base : base + start],
                            (((1,), (1,)), ((), ())),
                            preferred_element_type=F32,
                        )
                        if last:
                            out_ref[w, :, :start] = (acc[w, :, :start] + turned).astype(BF16)
                        else:
                            acc[w, :, :start] += turned
                base += size

    for k, name in order:
        run_stage(k, name)
    for copy in started:
        copy.wait_send()


def on_device(mesh_shape, factors, occ_energy, virt_energy, pairs):
    groups = mesh_shape["occ"]
    layers = mesh_shape["aux"] // (CORES * ROWS_Y)
    slab, depth, columns = factors.shape
    chunks, _ = plan_of(columns, layers)
    scratch = [
        pltpu.SMEM(pairs.shape, jnp.int32),
        pltpu.VMEM((1, slab), BF16),
        pltpu.VMEM((columns // LANES, LANES), F32),
        pltpu.SemaphoreType.DMA((3,)),
        pltpu.VMEM((slab, depth, columns), BF16),
        pltpu.VMEM((groups, 2 * slab, LANES), F32),
        pltpu.VMEM((depth, columns), BF16),
        pltpu.VMEM((depth, columns), BF16),
        pltpu.VMEM((columns, depth), BF16),
        pltpu.VMEM((columns, depth), BF16),
        pltpu.VMEM((2, depth, columns), F32),
    ]
    for chunk in chunks:
        rows, block = layout_of(chunk, layers)
        width = len(chunk) * LANES
        scratch += [
            pltpu.VMEM((2, rows, LANES), F32),
            pltpu.VMEM((2, rows // CORES, LANES), BF16),
            pltpu.VMEM((2, rows // CORES, LANES), BF16),
            pltpu.VMEM((2, rows // (CORES * ROWS_Y), LANES), BF16),
            pltpu.VMEM((2, rows // (CORES * ROWS_Y), LANES), BF16),
            pltpu.VMEM((2, layers, 2, block, LANES), BF16),
            pltpu.VMEM((CORES, ROWS_Y, layers, 2, block, LANES), BF16),
            pltpu.VMEM((rows, LANES), F32),
            pltpu.VMEM((rows, LANES), F32),
            pltpu.VMEM((groups - 1, depth, width), BF16),
            pltpu.VMEM((groups, depth, width), BF16),
        ]
    n = len(chunks)
    dma = pltpu.SemaphoreType.DMA
    scratch += [dma((n,))]
    scratch += [dma((groups,))] * 2
    scratch += [dma((groups, n))] * 2
    scratch += [dma((2, n))] * 2
    scratch += [dma((n, layers))] * 4
    scratch += [dma((2, n))] * 2
    vmem = pl.BlockSpec(memory_space=pltpu.VMEM)
    operands = (pairs, occ_energy[None], virt_energy.reshape(columns // LANES, LANES), factors)
    out = pl.pallas_call(
        functools.partial(body, groups, layers),
        out_shape=jax.ShapeDtypeStruct((2, depth, columns), BF16),
        in_specs=[pl.BlockSpec(memory_space=pltpu.HBM)] * 4,
        out_specs=vmem,
        scratch_shapes=scratch,
        compiler_params=pltpu.CompilerParams(
            collective_id=0, has_side_effects=True, vmem_limit_bytes=GRANT
        ),
    )(*[pltpu.with_memory_space_constraint(x, pltpu.HBM) for x in operands])
    return out[None]


def solution(mesh):
    in_specs = (P("occ", "aux", None), P("occ"), P(), P("occ", None))
    out_specs = P("occ", None, "aux", None)
    return jax.shard_map(
        functools.partial(on_device, dict(mesh.shape)),
        mesh=mesh,
        in_specs=in_specs,
        out_specs=out_specs,
        check_vma=False,
    )
```

```python
import functools

import jax
import jax.numpy as jnp
from jax import lax
from jax.experimental import pallas as pl
from jax.experimental.pallas import tpu as pltpu
from jax.sharding import PartitionSpec as P

LANES = 128
GRANT = 40 * 1024 * 1024
CORES = 2
ROWS_Y = 2
MESH = pl.DeviceIdType.MESH
F32 = jnp.float32
BF16 = jnp.bfloat16


def plan_of(columns, layers):
    strips = columns // LANES
    unit = CORES * ROWS_Y * layers * 16

    def fit(members):
        sizes = [(s + 1) * LANES for s in members]
        for at in reversed(range(len(members))):
            while sum(sizes) % unit and sizes[at] < columns:
                sizes[at] += LANES
        return [(s, (s + 1) * LANES, size) for s, size in zip(members, sizes)]

    split = [list(range(strips // 2))] + [[s] for s in range(strips // 2, strips)]
    chunks = [fit(members) for members in split]
    if any(sum(size for _, _, size in chunk) % unit for chunk in chunks):
        chunks = [fit(list(range(strips)))]
    stages = ["X", "C", "Y", "Z", "AZ", "AY", "AC"]
    when = {"X": 9, "C": 11, "Y": 15, "Z": 19, "AZ": 23, "AY": 27, "AC": 28}
    order = sorted((when[s] + 3 * k, k, stages.index(s), s) for s in stages for k in range(len(chunks)))
    return chunks, [(k, s) for _, k, _, s in order]


def layout_of(chunk, layers):
    rows = sum(size for _, _, size in chunk)
    return rows, rows // (CORES * ROWS_Y * layers)


def body(groups, layers, pairs_hbm, energy_hbm, virt_hbm, f_hbm, out_ref, *scratch):
    scratch = list(scratch)
    take = lambda: scratch.pop(0)
    slab, depth, columns = f_hbm.shape
    chunks, order = plan_of(columns, layers)
    pairs_ref, energy_ref, virt_ref, small_sem = [take() for _ in range(4)]
    f_ref, msgs, bi, bj, bi_t, bj_t, acc = [take() for _ in range(7)]
    per_chunk = [[take() for _ in range(11)] for _ in chunks]
    (f_sem, m_send, m_recv, x_send, x_recv, c_sem, y_sem, z_send, z_recv, az_send, az_recv, ay_send, ay_recv, ac_sem) = [
        take() for _ in range(14)
    ]

    aux = lax.axis_index("aux")
    occ = lax.axis_index("occ")
    core = lax.rem(aux, CORES)
    row = lax.rem(aux // CORES, ROWS_Y)
    layer = aux // (CORES * ROWS_Y)

    def device(z, y, c, g):
        return {"aux": (z * ROWS_Y + y) * CORES + c, "occ": g}

    core_peer = device(layer, row, 1 - core, occ)
    row_peer = device(layer, 1 - row, core, occ)
    layer_peer = lambda j: device(lax.rem(layer + j, layers), row, core, occ)
    occ_peer = lambda d: {"aux": aux, "occ": lax.rem(occ + groups - d, groups)}

    def columns_of(chunk):
        return slice(chunk[0][0] * LANES, chunk[-1][1])

    small = []
    for at, (src, dst) in enumerate([(pairs_hbm, pairs_ref), (energy_hbm, energy_ref), (virt_hbm, virt_ref)]):
        small.append(pltpu.make_async_copy(src, dst, small_sem.at[at]))
        small[at].start()
    loads = []
    for k, chunk in enumerate(chunks):
        cols = columns_of(chunk)
        loads.append(pltpu.make_async_copy(f_hbm.at[:, :, cols], f_ref.at[:, :, cols], f_sem.at[k]))
        loads[k].start()
    barrier = pltpu.get_barrier_semaphore()
    peers = [core_peer, row_peer]
    peers += [layer_peer(j) for j in range(1, layers)]
    peers += [occ_peer(d) for d in range(1, groups)]
    for peer in peers:
        pl.semaphore_signal(barrier, inc=1, device_id=peer, device_id_type=MESH)
    pl.semaphore_wait(barrier, len(peers))

    started = []

    def send(src, dst, send_sem, recv_sem, peer):
        copy = pltpu.make_async_remote_copy(
            src_ref=src, dst_ref=dst, send_sem=send_sem, recv_sem=recv_sem, device_id=peer, device_id_type=MESH
        )
        copy.start()
        started.append(copy)
        return copy

    def landed(ref, send_sem, recv_sem, peer):
        pltpu.make_async_remote_copy(
            src_ref=ref, dst_ref=ref, send_sem=send_sem, recv_sem=recv_sem, device_id=peer, device_id_type=MESH
        ).wait_recv()

    for copy in small:
        copy.wait()
    i_local = lax.rem(pairs_ref[0, 0], slab)
    j_slab = pairs_ref[0, 1] // slab
    j_local = pairs_ref[0, 1] - j_slab * slab
    distance = lax.rem(j_slab - occ + groups, groups)
    slab_energy = energy_ref[...].astype(F32)
    for o in range(slab):
        wants = jnp.where(j_local == o, 1.0, 0.0).astype(F32)
        msgs[0, o : o + 1, :] = jnp.full((1, LANES), wants, F32)
        msgs[0, slab + o : slab + o + 1, :] = jnp.broadcast_to(slab_energy[:, o : o + 1], (1, LANES))
    sent = [send(msgs.at[0], msgs.at[d], m_send.at[d], m_recv.at[d], occ_peer(d)) for d in range(1, groups)]
    for d in range(1, groups):
        sent[d - 1].wait_recv()

    for k, chunk in enumerate(chunks):
        loads[k].wait()
        cols = columns_of(chunk)
        stage, slots = per_chunk[k][9:11]
        for d in range(1, groups):
            asked = msgs[groups - d]
            rows = jnp.zeros((depth, cols.stop - cols.start), BF16)
            for o in range(slab):
                mask = jnp.concatenate([asked[o : o + 1]] * len(chunk), axis=1).astype(BF16)
                rows = rows + f_ref[o, :, cols] * mask
            stage[d - 1] = rows
            send(stage.at[d - 1], slots.at[d], x_send.at[d, k], x_recv.at[d, k], occ_peer(d))
    for k, chunk in enumerate(chunks):
        per_chunk[k][10][0] = f_ref[j_local, :, columns_of(chunk)]
    bi[...] = f_ref[i_local]
    bi_t[...] = bi[...].T
    energy = msgs[0, pl.ds(slab + i_local, 1), :] + msgs[distance, pl.ds(slab + j_local, 1), :]

    down = []
    for t in range(columns // LANES):
        down.append(jnp.broadcast_to(virt_ref[t : t + 1, :], (LANES, LANES)).T)
    for k, chunk in enumerate(chunks):
        part, v_rows, v_lanes = per_chunk[k][0], *per_chunk[k][7:9]
        base = 0
        for s, end, size in chunk:
            for t in range(size // LANES):
                v_rows[base + t * LANES : base + (t + 1) * LANES, :] = down[t]
            v_lanes[base : base + size, :] = jnp.broadcast_to(virt_ref[s : s + 1, :], (size, LANES))
            if size > end:
                part[:, base + end : base + size, :] = jnp.zeros((2, size - end, LANES), F32)
            base += size

    pending = {}

    def run_stage(k, name):
        chunk = chunks[k]
        part, give, got_c, give_y, got_y, give_z, amp, v_rows, v_lanes, stage, slots = per_chunk[k]
        rows, block = layout_of(chunk, layers)
        half, quarter = rows // CORES, rows // (CORES * ROWS_Y)

        def span(index, size):
            return pl.ds(pl.multiple_of(index * size, size), size)

        if name == "X":
            for d in range(1, groups):
                landed(slots.at[d], x_send.at[d, k], x_recv.at[d, k], occ_peer(d))
            cols = columns_of(chunk)
            arrived = slots[distance]
            bj[:, cols] = arrived
            bj_t[cols, :] = arrived.T
            base = 0
            for s, end, size in chunk:
                cols = slice(s * LANES, end)
                part[0, base : base + end, :] = jnp.dot(bi_t[:end, :], bj[:, cols], preferred_element_type=F32)
                part[1, base : base + end, :] = jnp.dot(bj_t[:end, :], bi[:, cols], preferred_element_type=F32)
                base += size
            give[...] = part[:, span(1 - core, half), :].astype(BF16)
            pending[k, "C"] = send(give, got_c, c_sem.at[0, k], c_sem.at[1, k], core_peer)
        elif name == "C":
            pending[k, "C"].wait_recv()
            there = span(core * ROWS_Y + 1 - row, quarter)
            here = span(core * ROWS_Y + row, quarter)
            give_y[...] = (part[:, there, :] + got_c[:, span(1 - row, quarter), :].astype(F32)).astype(BF16)
            pending[k, "Y"] = send(give_y, got_y, y_sem.at[0, k], y_sem.at[1, k], row_peer)
            part[:, here, :] = part[:, here, :] + got_c[:, span(row, quarter), :].astype(F32)
        elif name == "Y":
            pending[k, "Y"].wait_recv()
            base = (core * ROWS_Y + row) * layers
            for j in range(1, layers):
                z = lax.rem(layer + j, layers)
                give_z[0, j] = (part[:, span(base + z, block), :] + got_y[:, span(z, block), :].astype(F32)).astype(BF16)
                send(give_z.at[0, j], give_z.at[1, j], z_send.at[k, j], z_recv.at[k, j], layer_peer(j))
        elif name == "Z":
            mine = span((core * ROWS_Y + row) * layers + layer, block)
            total = part[:, mine, :] + got_y[:, span(layer, block), :].astype(F32)
            down_rows = v_rows[mine, :]
            along = v_lanes[mine, :]
            for j in range(1, layers):
                landed(give_z.at[1, j], z_send.at[k, j], z_recv.at[k, j], layer_peer(j))
                total = total + give_z[1, j].astype(F32)
            first = (2.0 * total[0] - total[1]) / (energy - down_rows - along)
            second = (2.0 * total[1] - total[0]) / (energy - along - down_rows)
            amp[core, row, layer, 0] = first.astype(BF16)
            amp[core, row, layer, 1] = second.astype(BF16)
            home = amp.at[core, row, layer]
            for j in range(1, layers):
                send(home, home, az_send.at[k, j], az_recv.at[k, j], layer_peer(j))
            send(home, home, ay_send.at[k, 0], ay_recv.at[k, 0], row_peer)
        elif name == "AZ":
            for j in range(1, layers):
                z = lax.rem(layer + layers - j, layers)
                block_ref = amp.at[core, row, z]
                landed(block_ref, az_send.at[k, j], az_recv.at[k, j], layer_peer(j))
                send(block_ref, block_ref, ay_send.at[k, j], ay_recv.at[k, j], row_peer)
            home = amp.at[core, row]
            send(home, home, ac_sem.at[0, k, 0], ac_sem.at[1, k, 0], core_peer)
        elif name == "AY":
            for j in range(layers):
                z = lax.rem(layer + layers - j, layers)
                landed(amp.at[core, 1 - row, z], ay_send.at[k, j], ay_recv.at[k, j], row_peer)
            home = amp.at[core, 1 - row]
            send(home, home, ac_sem.at[0, k, 1], ac_sem.at[1, k, 1], core_peer)
        else:
            landed(amp.at[1 - core, row], ac_sem.at[0, k, 0], ac_sem.at[1, k, 0], core_peer)
            landed(amp.at[1 - core, 1 - row], ac_sem.at[0, k, 1], ac_sem.at[1, k, 1], core_peer)
            whole = [amp[:, :, :, w].reshape(rows, LANES) for w in range(2)]
            base = 0
            for s, end, size in chunk:
                start = s * LANES
                cols = slice(start, end)
                last = end == columns
                for w in range(2):
                    b = bj if w == 0 else bi
                    plain = jnp.dot(b[:, :end], whole[1 - w][base : base + end], preferred_element_type=F32)
                    if last:
                        out_ref[w, :, cols] = plain.astype(BF16)
                    else:
                        acc[w, :, cols] = plain
                    if start:
                        turned = lax.dot_general(
                            b[:, cols],
                            whole[w][base : base + start],
                            (((1,), (1,)), ((), ())),
                            preferred_element_type=F32,
                        )
                        if last:
                            out_ref[w, :, :start] = (acc[w, :, :start] + turned).astype(BF16)
                        else:
                            acc[w, :, :start] += turned
                base += size

    for k, name in order:
        run_stage(k, name)
    for copy in started:
        copy.wait_send()


def on_device(mesh_shape, factors, occ_energy, virt_energy, pairs):
    groups = mesh_shape["occ"]
    layers = mesh_shape["aux"] // (CORES * ROWS_Y)
    slab, depth, columns = factors.shape
    chunks, _ = plan_of(columns, layers)
    scratch = [
        pltpu.SMEM(pairs.shape, jnp.int32),
        pltpu.VMEM((1, slab), BF16),
        pltpu.VMEM((columns // LANES, LANES), F32),
        pltpu.SemaphoreType.DMA((3,)),
        pltpu.VMEM((slab, depth, columns), BF16),
        pltpu.VMEM((groups, 2 * slab, LANES), F32),
        pltpu.VMEM((depth, columns), BF16),
        pltpu.VMEM((depth, columns), BF16),
        pltpu.VMEM((columns, depth), BF16),
        pltpu.VMEM((columns, depth), BF16),
        pltpu.VMEM((2, depth, columns), F32),
    ]
    for chunk in chunks:
        rows, block = layout_of(chunk, layers)
        width = len(chunk) * LANES
        scratch += [
            pltpu.VMEM((2, rows, LANES), F32),
            pltpu.VMEM((2, rows // CORES, LANES), BF16),
            pltpu.VMEM((2, rows // CORES, LANES), BF16),
            pltpu.VMEM((2, rows // (CORES * ROWS_Y), LANES), BF16),
            pltpu.VMEM((2, rows // (CORES * ROWS_Y), LANES), BF16),
            pltpu.VMEM((2, layers, 2, block, LANES), BF16),
            pltpu.VMEM((CORES, ROWS_Y, layers, 2, block, LANES), BF16),
            pltpu.VMEM((rows, LANES), F32),
            pltpu.VMEM((rows, LANES), F32),
            pltpu.VMEM((groups - 1, depth, width), BF16),
            pltpu.VMEM((groups, depth, width), BF16),
        ]
    n = len(chunks)
    dma = pltpu.SemaphoreType.DMA
    scratch += [dma((n,))]
    scratch += [dma((groups,))] * 2
    scratch += [dma((groups, n))] * 2
    scratch += [dma((2, n))] * 2
    scratch += [dma((n, layers))] * 6
    scratch += [dma((2, n, 2))]
    vmem = pl.BlockSpec(memory_space=pltpu.VMEM)
    operands = (pairs, occ_energy[None], virt_energy.reshape(columns // LANES, LANES), factors)
    out = pl.pallas_call(
        functools.partial(body, groups, layers),
        out_shape=jax.ShapeDtypeStruct((2, depth, columns), BF16),
        in_specs=[pl.BlockSpec(memory_space=pltpu.HBM)] * 4,
        out_specs=vmem,
        scratch_shapes=scratch,
        compiler_params=pltpu.CompilerParams(
            collective_id=0, has_side_effects=True, vmem_limit_bytes=GRANT
        ),
    )(*[pltpu.with_memory_space_constraint(x, pltpu.HBM) for x in operands])
    return out[None]


def solution(mesh):
    in_specs = (P("occ", "aux", None), P("occ"), P(), P("occ", None))
    out_specs = P("occ", None, "aux", None)
    return jax.shard_map(
        functools.partial(on_device, dict(mesh.shape)),
        mesh=mesh,
        in_specs=in_specs,
        out_specs=out_specs,
        check_vma=False,
    )
```
